32 devices in a mesh: docs: 4 (over y, x), seg: 8 (over z, core).
Axes of the slice: x: 2, y: 2, z: 4, core: 2. Of those that a mesh axis runs over, the one named last changes fastest.
Arguments:
- tokens: bfloat16 [4, 4096, 768], P('docs', 'seg'), may hold values from -6 to 6
- cotangent: bfloat16 [4, 4096, 768], P('docs', 'seg'), may hold values from -6 to 6
- document_ids: int32 [4, 32], P('docs'), may hold values from 0 to 2, never falling along the last dimension, each value on 1 to 16 neighbouring positions
- inner_project: bfloat16 [768, 2304], P('seg'), may hold values from -0.21875 to 0.21875
- inner_output: bfloat16 [768, 768], P('seg'), may hold values from -0.875 to 0.875
- inner_expand: bfloat16 [768, 3072], P('seg'), may hold values from -0.21875 to 0.21875
- inner_shrink: bfloat16 [3072, 768], P('seg'), may hold values from -0.109375 to 0.109375
- inner_gains: float32 [2, 768], replicated, may hold values from 0.5 to 1.5
- inner_shifts: float32 [2, 768], replicated, may hold values from -3 to 3
- outer_project: bfloat16 [768, 2304], P('seg'), may hold values from -0.21875 to 0.21875
- outer_output: bfloat16 [768, 768], P('seg'), may hold values from -0.875 to 0.875
- outer_expand: bfloat16 [768, 3072], P('seg'), may hold values from -0.21875 to 0.21875
- outer_shrink: bfloat16 [3072, 768], P('seg'), may hold values from -0.109375 to 0.109375
- outer_gains: float32 [2, 768], replicated, may hold values from 0.5 to 1.5
- outer_shifts: float32 [2, 768], replicated, may hold values from -3 to 3
- position_table: bfloat16 [64, 768], replicated, may hold values from -3 to 3
Outputs:
- layer_output: bfloat16 [4, 4096, 768], P('docs', 'seg')
- tokens_grad: float32 [4, 4096, 768], P('docs', 'seg')
- inner_project_grad: float32 [768, 2304], P('seg')
- inner_output_grad: float32 [768, 768], P('seg')
- inner_expand_grad: float32 [768, 3072], P('seg')
- inner_shrink_grad: float32 [3072, 768], P('seg')
- inner_gains_grad: float32 [2, 768], P(None, 'seg')
- inner_shifts_grad: float32 [2, 768], P(None, 'seg')
- outer_project_grad: float32 [768, 2304], P('seg')
- outer_output_grad: float32 [768, 768], P('seg')
- outer_expand_grad: float32 [768, 3072], P('seg')
- outer_shrink_grad: float32 [3072, 768], P('seg')
- outer_gains_grad: float32 [2, 768], P(None, 'seg')
- outer_shifts_grad: float32 [2, 768], P(None, 'seg')
- position_table_grad: float32 [64, 768], P('seg')
The draws below stay inside these ranges and needn't reach their ends.
Inputs may be any that keep to these rules, and one draw needn't show every extreme that they name: `document_ids`: in each group the document ids never fall along the segments, every id of 0 to 2 occurs, each document has 1 to 16 segments and some document has exactly 16.
All inputs are finite; a program needn't handle non-finite values.
Results may differ from the reference program's by a relative error of at most 0.025.
Values may be sent and summed in bfloat16 or wider, within the bound.
No kernel may reach another device: no remote copies, remote signals or barrier semaphores. Data moves between devices by JAX's collectives and lax.ppermute only.
A program may use at most 192 MiB of HBM per device.

```python
import math
import jax
import jax.numpy as jnp
import numpy as np
from jax import lax

D = 768
HEADS = 12
HEAD_DIM = 64
FF = 3072
SEG_LEN = 128
MAX_SEGS = 64
SEG_DEV = 4
SEGS_GROUP = 32
GROUP_TOK = 4096
GROUPS = 4
DOCS_GROUP = 3
LONGEST = 16
N_DOCS = 4


def block_scale(rng, dims, shards, smallest, top_value):
    level, own = 1.0, jax.random.fold_in(rng, 6)
    for dim, shards_of in shards:
        draws = jnp.exp(jax.random.uniform(jax.random.fold_in(own, dim), (shards_of,), jnp.float32, smallest / len(shards), top_value / len(shards)))
        level = level * jnp.repeat(draws, dims[dim] // shards_of).reshape([-1 if axis == dim else 1 for axis in range(len(dims))])
    return level


def split_up(count, total, reach, slope):
    portions = [(1 << 20) // math.isqrt(grade ** slope) + 1 for grade in range(2, count + 1)]
    spare, holding = total - reach - (count - 1), [1] * (count - 1)
    while spare > 0:
        movable = [i for i in range(count - 1) if holding[i] < reach]
        whole, remaining = sum([portions[i] for i in movable]), spare
        for i in movable:
            addition = min(reach - holding[i], max(1, remaining * portions[i] // whole), spare)
            holding[i] = holding[i] + addition
            spare = spare - addition
    return np.array([reach] + holding)


def ragged_sizes(own_key, amount, total, limit, slope):
    if amount == 2:
        one = jax.random.randint(own_key, (), max(1, total - limit), min(limit, total - 1) + 1)
        return jnp.stack([one, total - one])
    sizes = jnp.asarray(split_up(amount, total, limit, slope), jnp.int32)
    twos = (amount - 1) // 2
    donor, receiver = sizes[1:1 + 2 * twos:2], sizes[2:2 + 2 * twos:2]
    room = jnp.minimum(donor - 1, limit - receiver)
    moved = jax.random.randint(jax.random.fold_in(own_key, 1), (twos,), 0, 1 << 20) % (room + 1)
    sizes = sizes.at[1:1 + 2 * twos:2].set(donor - moved).at[2:2 + 2 * twos:2].set(receiver + moved)
    return sizes[jax.random.permutation(jax.random.fold_in(own_key, 2), amount)]


def normal_values(stream_key, shape, scale, bound, split=(), kind=jnp.bfloat16):
    array = jax.random.normal(stream_key, shape, jnp.float32) * scale
    if len(split) > 0:
        array = block_scale(stream_key, shape, split, -0.22, 0.18) * array
    return jnp.clip(array, min=-bound, max=bound).astype(kind)


def setup_inputs(seed: int = 0) -> dict:
    splits = jax.random.split(jax.random.key(seed), 17)
    tokens = normal_values(splits[0], (GROUPS, GROUP_TOK, D), 1.0, 6.0, ((0, 4), (1, 8)))
    cotangent = normal_values(splits[1], (GROUPS, GROUP_TOK, D), 1.0, 6.0, ((0, 4), (1, 8)))
    document_ids = jax.vmap(lambda own: jnp.searchsorted(jnp.cumsum(ragged_sizes(own, DOCS_GROUP, SEGS_GROUP, LONGEST, 2)), jnp.arange(SEGS_GROUP), side="right"))(jax.random.split(splits[2], GROUPS)).reshape((GROUPS, SEGS_GROUP)).astype(jnp.int32)
    inner_project = normal_values(splits[3], (D, 3 * D), D ** -0.5, 0.21875, ((0, 8),))
    inner_output = normal_values(splits[4], (D, D), (D // 16) ** -0.5, 0.875, ((0, 8),))
    inner_expand = normal_values(splits[5], (D, FF), D ** -0.5, 0.21875, ((0, 8),))
    inner_shrink = normal_values(splits[6], (FF, D), FF ** -0.5, 0.109375, ((0, 8),))
    inner_gains = jnp.clip(1.0 + 0.1 * jax.random.normal(splits[7], (2, D), jnp.float32), 0.5, 1.5)
    inner_shifts = normal_values(splits[8], (2, D), 0.5, 3.0, (), jnp.float32)
    outer_project = normal_values(splits[9], (D, 3 * D), D ** -0.5, 0.21875, ((0, 8),))
    outer_output = normal_values(splits[10], (D, D), (D // 16) ** -0.5, 0.875, ((0, 8),))
    outer_expand = normal_values(splits[11], (D, FF), D ** -0.5, 0.21875, ((0, 8),))
    outer_shrink = normal_values(splits[12], (FF, D), FF ** -0.5, 0.109375, ((0, 8),))
    outer_gains = jnp.clip(1.0 + 0.1 * jax.random.normal(splits[13], (2, D), jnp.float32), 0.5, 1.5)
    outer_shifts = normal_values(splits[14], (2, D), 0.5, 3.0, (), jnp.float32)
    position_table = normal_values(splits[15], (MAX_SEGS, D), 0.5, 3.0)
    return {"tokens": tokens, "cotangent": cotangent, "document_ids": document_ids, "inner_project": inner_project, "inner_output": inner_output, "inner_expand": inner_expand, "inner_shrink": inner_shrink, "inner_gains": inner_gains, "inner_shifts": inner_shifts, "outer_project": outer_project, "outer_output": outer_output, "outer_expand": outer_expand, "outer_shrink": outer_shrink, "outer_gains": outer_gains, "outer_shifts": outer_shifts, "position_table": position_table}


EPS = 1e-05
HIGH = lax.Precision.HIGHEST

@jax.custom_vjp
def low(v):
    return lax.optimization_barrier(v.astype(jnp.bfloat16)).astype(jnp.float32)

@jax.custom_vjp
def low_back(v):
    return v

def low_keep(v):
    return (low(v), None)

def low_pass(kept, grad):
    return (grad,)

def back_keep(v):
    return (v, None)

def back_low(kept, grad):
    return (low(grad),)
low.defvjp(low_keep, low_pass)
low_back.defvjp(back_keep, back_low)

def product(left, right):
    return jnp.dot(left, right, precision=HIGH)

def normalize(resid, gain, shift):
    center = resid - lax.optimization_barrier(jnp.mean(resid, axis=-1, keepdims=True))
    spread = lax.optimization_barrier(jnp.mean(center * center, axis=-1, keepdims=True))
    return center * lax.rsqrt(spread + EPS) * gain + shift

def attend(query, keys, values, allowed):
    shape = query.shape
    query = query.reshape(shape[0], shape[1], HEADS, HEAD_DIM)
    keys = keys.reshape(shape[0], shape[1], HEADS, HEAD_DIM)
    values = values.reshape(shape[0], shape[1], HEADS, HEAD_DIM)
    scores = low_back(jnp.einsum('gqhe,gkhe->ghqk', query, keys, precision=HIGH) * HEAD_DIM ** (-0.5))
    scores = jnp.where(allowed, scores, -1000000000.0)
    chance = low(jax.nn.softmax(scores, axis=-1))
    mixed = jnp.einsum('ghqk,gkhe->gqhe', chance, values, precision=HIGH)
    return mixed.reshape(shape)

def block(resid_in, product_in, weights, allowed):
    project, output, expand, shrink, gains, shifts = weights
    width = resid_in.shape[-1]
    triple = low(low_back(product(product_in, project)))
    query = triple[..., :width]
    keys = triple[..., width:2 * width]
    values = triple[..., 2 * width:]
    mixed = low(low_back(attend(query, keys, values, allowed)))
    branch = low_back(product(mixed, output))
    first = normalize(resid_in + branch, gains[0], shifts[0])
    hidden = low_back(product(low(first), expand))
    active = low(jax.nn.gelu(hidden, approximate=False))
    second = first + low_back(product(active, shrink))
    return normalize(second, gains[1], shifts[1])

def places_of(doc_row):
    count = doc_row.shape[0]
    before = lax.optimization_barrier(jnp.sum((doc_row[None, :] < doc_row[:, None]).astype(jnp.int32), axis=1))
    return jnp.arange(count, dtype=jnp.int32) - before

def forward(tokens, inner, outer, table, document_ids, places):
    segments = tokens.reshape(-1, SEG_DEV, SEG_LEN, D)
    whole = jnp.ones((1, 1, SEG_LEN, SEG_LEN), dtype=jnp.bool_)

    def inner_step(piece):
        return block(piece, piece, inner, whole)
    settled = lax.map(jax.checkpoint(inner_step), segments)
    settled = settled.reshape(N_DOCS, SEGS_GROUP, SEG_LEN, D)
    summary = low(settled[:, :, 0, :]) + table[places]

    def outer_step(pair):
        rows, doc_row = pair
        allowed = (doc_row[:, None] == doc_row[None, :])[None, None]
        return block(rows[None], low(rows[None]), outer, allowed)[0]
    merged = lax.map(jax.checkpoint(outer_step), (summary, document_ids))
    result = settled.at[:, :, 0, :].set(merged)
    return result.reshape(N_DOCS, SEGS_GROUP * SEG_LEN, D)

def reference(tokens, cotangent, document_ids, inner_project, inner_output, inner_expand, inner_shrink, inner_gains, inner_shifts, outer_project, outer_output, outer_expand, outer_shrink, outer_gains, outer_shifts, position_table):
    places = jax.vmap(places_of)(document_ids)
    inner = tuple((item.astype(jnp.float32) for item in (inner_project, inner_output, inner_expand, inner_shrink, inner_gains, inner_shifts)))
    outer = tuple((item.astype(jnp.float32) for item in (outer_project, outer_output, outer_expand, outer_shrink, outer_gains, outer_shifts)))

    def run(tokens_f, inner_w, outer_w, table):
        return forward(tokens_f, inner_w, outer_w, table, document_ids, places)
    result, pullback = jax.vjp(run, tokens.astype(jnp.float32), inner, outer, position_table.astype(jnp.float32))
    token_grad, inner_grad, outer_grad, table_grad = pullback(cotangent.astype(jnp.float32))
    return (result.astype(jnp.bfloat16), token_grad, inner_grad[0], inner_grad[1], inner_grad[2], inner_grad[3], inner_grad[4], inner_grad[5], outer_grad[0], outer_grad[1], outer_grad[2], outer_grad[3], outer_grad[4], outer_grad[5], table_grad)
```

```python
import jax
import jax.numpy as jnp
from jax import lax
from jax.sharding import PartitionSpec as P

HEADS = 12
HEAD_DIM = 64
SEG_LEN = 128


EPS = 1e-05
HIGH = lax.Precision.HIGHEST
LOWEST = -1000000000.0


def forward_dot(left, right):
    return jnp.dot(left, right, preferred_element_type=jnp.float32)


def across_dot(left, right):
    return lax.dot_general(
        left, right, (((0,), (0,)), ((), ())), preferred_element_type=jnp.float32
    )


def against_dot(left, right):
    return lax.dot_general(
        left, right, (((1,), (1,)), ((), ())), preferred_element_type=jnp.float32
    )


def table_sum(onehot, grad):
    return lax.dot_general(onehot, grad, (((0,), (0,)), ((), ())), precision=HIGH)


def norm_forward(resid, gain, shift):
    center = resid - jnp.mean(resid, axis=-1, keepdims=True)
    inverse = lax.rsqrt(jnp.mean(center * center, axis=-1, keepdims=True) + EPS)
    normed = center * inverse
    return (normed * gain + shift, normed, inverse)


def norm_backward(grad, normed, inverse, gain):
    scaled = grad * gain
    resid_grad = inverse * (
        scaled
        - jnp.mean(scaled, axis=-1, keepdims=True)
        - normed * jnp.mean(scaled * normed, axis=-1, keepdims=True)
    )
    return (resid_grad, jnp.sum(grad * normed, axis=0), jnp.sum(grad, axis=0))


def split_heads(matrix):
    return matrix.reshape(matrix.shape[0], matrix.shape[1], HEADS, HEAD_DIM)


def scores_of(query, keys, allowed):
    scores = jnp.einsum(
        "gqhe,gkhe->ghqk", split_heads(query), split_heads(keys), preferred_element_type=jnp.float32
    ) * HEAD_DIM ** (-0.5)
    if allowed is None:
        return scores
    return jnp.where(allowed[:, None], scores, LOWEST)


def attend_forward(query, keys, values, allowed):
    scores = scores_of(query, keys, allowed)
    peak = jnp.max(scores, axis=-1, keepdims=True)
    raised = jnp.exp(scores - peak)
    total = jnp.sum(raised, axis=-1, keepdims=True)
    chance = (raised / total).astype(jnp.bfloat16)
    mixed = jnp.einsum(
        "ghqk,gkhe->gqhe", chance, split_heads(values), preferred_element_type=jnp.float32
    )
    return (mixed.reshape(query.shape).astype(jnp.bfloat16), peak + jnp.log(total))


def attend_backward(mixed_grad, query, keys, values, allowed, log_total):
    chance = jnp.exp(scores_of(query, keys, allowed) - log_total)
    grad_heads = split_heads(mixed_grad)
    values_grad = jnp.einsum(
        "ghqk,gqhe->gkhe",
        chance.astype(jnp.bfloat16),
        grad_heads,
        preferred_element_type=jnp.float32,
    )
    chance_grad = jnp.einsum(
        "gqhe,gkhe->ghqk", grad_heads, split_heads(values), preferred_element_type=jnp.float32
    )
    scores_grad = (
        chance * (chance_grad - jnp.sum(chance * chance_grad, axis=-1, keepdims=True))
    ).astype(jnp.bfloat16)
    query_grad = jnp.einsum(
        "ghqk,gkhe->gqhe", scores_grad, split_heads(keys), preferred_element_type=jnp.float32
    ) * HEAD_DIM ** (-0.5)
    keys_grad = jnp.einsum(
        "ghqk,gqhe->gkhe", scores_grad, split_heads(query), preferred_element_type=jnp.float32
    ) * HEAD_DIM ** (-0.5)
    return (
        query_grad.reshape(query.shape),
        keys_grad.reshape(keys.shape),
        values_grad.reshape(values.shape),
    )


def gelu_slope(hidden):
    return (
        0.5 * (1.0 + lax.erf(hidden * 0.7071067811865476))
        + hidden * jnp.exp(-0.5 * hidden * hidden) * 0.3989422804014327
    )


def tail_forward(resid, mixed, output, expand, shrink, gains, shifts):
    first, normed_one, inverse_one = norm_forward(
        resid + forward_dot(mixed, output), gains[0], shifts[0]
    )
    first_low = first.astype(jnp.bfloat16)
    hidden = forward_dot(first_low, expand)
    active = jax.nn.gelu(hidden, approximate=False).astype(jnp.bfloat16)
    second, normed_two, inverse_two = norm_forward(
        first + forward_dot(active, shrink), gains[1], shifts[1]
    )
    return (second, (normed_one, inverse_one, first_low, hidden, active, normed_two, inverse_two))


def tail_backward(grad, kept, output, expand, shrink, gains):
    normed_one, inverse_one, first_low, hidden, active, normed_two, inverse_two = kept
    second_grad, gain_two, shift_two = norm_backward(grad, normed_two, inverse_two, gains[1])
    branch_low = second_grad.astype(jnp.bfloat16)
    hidden_grad = (against_dot(branch_low, shrink) * gelu_slope(hidden)).astype(jnp.bfloat16)
    first_grad, gain_one, shift_one = norm_backward(
        second_grad + against_dot(hidden_grad, expand), normed_one, inverse_one, gains[0]
    )
    attend_low = first_grad.astype(jnp.bfloat16)
    mixed_grad = against_dot(attend_low, output).astype(jnp.bfloat16)
    return (
        first_grad,
        mixed_grad,
        (branch_low, hidden_grad, attend_low),
        jnp.stack([gain_one, gain_two]),
        jnp.stack([shift_one, shift_two]),
    )


def tail_mats(mixed, kept, factors):
    branch_low, hidden_grad, attend_low = factors
    return (
        across_dot(mixed, attend_low),
        across_dot(kept[2], hidden_grad),
        across_dot(kept[4], branch_low),
    )


def gather_whole(shard):
    own_rows = shard.shape[0] // lax.axis_size("docs")
    part = lax.dynamic_slice_in_dim(shard, lax.axis_index("docs") * own_rows, own_rows)
    return lax.all_gather(part, ("seg", "docs"), axis=0, tiled=True)


def sum_scatter(partial):
    part = lax.psum_scatter(
        partial.astype(jnp.bfloat16), ("seg", "docs"), scatter_dimension=0, tiled=True
    )
    return lax.all_gather(part, "docs", axis=0, tiled=True).astype(jnp.float32)


def per_device(
    tokens,
    cotangent,
    document_ids,
    inner_project,
    inner_output,
    inner_expand,
    inner_shrink,
    inner_gains,
    inner_shifts,
    outer_project,
    outer_output,
    outer_expand,
    outer_shrink,
    outer_gains,
    outer_shifts,
    position_table,
):
    rows = tokens.shape[1]
    width = tokens.shape[2]
    local_segs = rows // SEG_LEN
    parts = lax.axis_size("seg")
    groups = lax.axis_size("docs")
    here = lax.axis_index("seg")
    group = lax.axis_index("docs")
    inner = tuple(
        gather_whole(w) for w in (inner_project, inner_output, inner_expand, inner_shrink)
    )
    source = tokens[0]
    triple = (
        forward_dot(source, inner[0]).astype(jnp.bfloat16).reshape(local_segs, SEG_LEN, 3 * width)
    )
    query = triple[..., :width]
    keys = triple[..., width : 2 * width]
    values = triple[..., 2 * width :]
    mixed, log_total = attend_forward(query, keys, values, None)
    mixed = mixed.reshape(rows, width)
    settled, kept = tail_forward(
        source.astype(jnp.float32), mixed, inner[1], inner[2], inner[3], inner_gains, inner_shifts
    )
    framed = settled.reshape(local_segs, SEG_LEN, width)
    summary_own = framed[:, 0, :].astype(jnp.bfloat16)
    cot_frames = cotangent[0].reshape(local_segs, SEG_LEN, width)
    summary_cot = cot_frames[:, 0, :]
    doc_all = lax.all_gather(document_ids, "docs", axis=0, tiled=True)
    count = doc_all.shape[1]
    before = jnp.sum((doc_all[:, None, :] < doc_all[:, :, None]).astype(jnp.int32), axis=2)
    places = (jnp.arange(count, dtype=jnp.int32)[None] - before).reshape(groups * count)
    onehot = (
        places[:, None] == jnp.arange(position_table.shape[0], dtype=jnp.int32)[None, :]
    ).astype(jnp.float32)
    outer = tuple(
        gather_whole(w) for w in (outer_project, outer_output, outer_expand, outer_shrink)
    )
    start = group * count + here * local_segs
    mat_rows = width // parts
    table_rows = position_table.shape[0] // parts
    both = lax.all_gather(
        jnp.concatenate([summary_own, summary_cot], axis=1), ("docs", "seg"), axis=0, tiled=True
    )
    summary_all = both[:, :width]
    cot_all = both[:, width:]
    allowed = doc_all[:, :, None] == doc_all[:, None, :]
    resid = summary_all.astype(jnp.float32) + forward_dot(
        onehot.astype(jnp.bfloat16), position_table
    )
    resid_low = resid.astype(jnp.bfloat16)
    outer_triple = (
        forward_dot(resid_low, outer[0]).astype(jnp.bfloat16).reshape(groups, count, 3 * width)
    )
    outer_query = outer_triple[..., :width]
    outer_keys = outer_triple[..., width : 2 * width]
    outer_values = outer_triple[..., 2 * width :]
    outer_mixed, outer_total = attend_forward(outer_query, outer_keys, outer_values, allowed)
    outer_mixed = outer_mixed.reshape(groups * count, width)
    merged_all, outer_kept = tail_forward(
        resid, outer_mixed, outer[1], outer[2], outer[3], outer_gains, outer_shifts
    )
    back_resid, back_mixed, outer_factors, outer_gain_grad, outer_shift_grad = tail_backward(
        cot_all.astype(jnp.float32), outer_kept, outer[1], outer[2], outer[3], outer_gains
    )
    query_grad, keys_grad, values_grad = attend_backward(
        back_mixed.reshape(groups, count, width),
        outer_query,
        outer_keys,
        outer_values,
        allowed,
        outer_total,
    )
    outer_triple_grad = (
        jnp.concatenate([query_grad, keys_grad, values_grad], axis=2)
        .astype(jnp.bfloat16)
        .reshape(groups * count, 3 * width)
    )
    summary_all_grad = back_resid + against_dot(outer_triple_grad, outer[0])
    merged = lax.dynamic_slice_in_dim(merged_all, start, local_segs)
    summary_grad = lax.dynamic_slice_in_dim(summary_all_grad, start, local_segs)
    branch_low, hidden_grad, attend_low = outer_factors

    def own(matrix):
        each = matrix.shape[1] // parts
        return lax.dynamic_slice_in_dim(matrix, here * each, each, axis=1)

    outer_grads = (
        across_dot(own(resid_low), outer_triple_grad),
        across_dot(own(outer_mixed), attend_low),
        across_dot(own(outer_kept[2]), hidden_grad),
        across_dot(own(outer_kept[4]), branch_low),
        own(outer_gain_grad),
        own(outer_shift_grad),
        table_sum(own(onehot), summary_all_grad),
    )
    layer_output = framed.at[:, 0, :].set(merged).reshape(rows, width).astype(jnp.bfloat16)
    tail_grad = cot_frames.astype(jnp.float32).at[:, 0, :].set(summary_grad).reshape(rows, width)
    first_grad, mixed_grad, inner_factors, inner_gain_grad, inner_shift_grad = tail_backward(
        tail_grad, kept, inner[1], inner[2], inner[3], inner_gains
    )
    inner_mats = tail_mats(mixed, kept, inner_factors)
    query_grad, keys_grad, values_grad = attend_backward(
        mixed_grad.reshape(local_segs, SEG_LEN, width), query, keys, values, None, log_total
    )
    triple_grad = (
        jnp.concatenate([query_grad, keys_grad, values_grad], axis=2)
        .reshape(rows, 3 * width)
        .astype(jnp.bfloat16)
    )
    tokens_grad = first_grad + against_dot(triple_grad, inner[0])
    small = lax.psum(
        jnp.concatenate([inner_gain_grad, inner_shift_grad], axis=0), ("docs", "seg")
    )
    small = own(small)
    return (
        layer_output[None],
        tokens_grad[None],
        sum_scatter(across_dot(source, triple_grad)),
        sum_scatter(inner_mats[0]),
        sum_scatter(inner_mats[1]),
        sum_scatter(inner_mats[2]),
        small[:2],
        small[2:],
    ) + outer_grads


def solution(mesh):
    placed = (
        P("docs", "seg", None),
        P("docs", "seg", None),
        P("docs", None),
        P("seg", None),
        P("seg", None),
        P("seg", None),
        P("seg", None),
        P(),
        P(),
        P("seg", None),
        P("seg", None),
        P("seg", None),
        P("seg", None),
        P(),
        P(),
        P(),
    )
    return jax.shard_map(
        per_device,
        mesh=mesh,
        in_specs=placed,
        out_specs=(
            P("docs", "seg", None),
            P("docs", "seg", None),
            P("seg", None),
            P("seg", None),
            P("seg", None),
            P("seg", None),
            P(None, "seg"),
            P(None, "seg"),
            P("seg", None),
            P("seg", None),
            P("seg", None),
            P("seg", None),
            P(None, "seg"),
            P(None, "seg"),
            P("seg", None),
        ),
        check_vma=False,
    )
```

```python
import jax
import jax.numpy as jnp
from jax import lax
from jax.experimental import pallas as pl
from jax.experimental.pallas import tpu as pltpu
from jax.sharding import PartitionSpec as P

HEADS = 12
HEAD_DIM = 64
SEG_LEN = 128


EPS = 1e-05
HIGH = lax.Precision.HIGHEST
LOWEST = -1000000000.0


def forward_dot(left, right):
    return jnp.dot(left, right, preferred_element_type=jnp.float32)


def across_dot(left, right):
    return lax.dot_general(
        left, right, (((0,), (0,)), ((), ())), preferred_element_type=jnp.float32
    )


def against_dot(left, right):
    return lax.dot_general(
        left, right, (((1,), (1,)), ((), ())), preferred_element_type=jnp.float32
    )


def table_sum(onehot, grad):
    return lax.dot_general(onehot, grad, (((0,), (0,)), ((), ())), precision=HIGH)


def norm_forward(resid, gain, shift):
    center = resid - jnp.mean(resid, axis=-1, keepdims=True)
    inverse = lax.rsqrt(jnp.mean(center * center, axis=-1, keepdims=True) + EPS)
    normed = center * inverse
    return (normed * gain + shift, normed, inverse)


def norm_backward(grad, normed, inverse, gain):
    scaled = grad * gain
    resid_grad = inverse * (
        scaled
        - jnp.mean(scaled, axis=-1, keepdims=True)
        - normed * jnp.mean(scaled * normed, axis=-1, keepdims=True)
    )
    return (resid_grad, jnp.sum(grad * normed, axis=0), jnp.sum(grad, axis=0))


def split_heads(matrix):
    return matrix.reshape(matrix.shape[0], matrix.shape[1], HEADS, HEAD_DIM)


def scores_of(query, keys, allowed):
    scores = jnp.einsum(
        "gqhe,gkhe->ghqk", split_heads(query), split_heads(keys), preferred_element_type=jnp.float32
    ) * HEAD_DIM ** (-0.5)
    if allowed is None:
        return scores
    return jnp.where(allowed[:, None], scores, LOWEST)


def attend_forward(query, keys, values, allowed):
    scores = scores_of(query, keys, allowed)
    peak = jnp.max(scores, axis=-1, keepdims=True)
    raised = jnp.exp(scores - peak)
    total = jnp.sum(raised, axis=-1, keepdims=True)
    chance = (raised / total).astype(jnp.bfloat16)
    mixed = jnp.einsum(
        "ghqk,gkhe->gqhe", chance, split_heads(values), preferred_element_type=jnp.float32
    )
    return (mixed.reshape(query.shape).astype(jnp.bfloat16), peak + jnp.log(total))


def attend_backward(mixed_grad, query, keys, values, allowed, log_total):
    chance = jnp.exp(scores_of(query, keys, allowed) - log_total)
    grad_heads = split_heads(mixed_grad)
    values_grad = jnp.einsum(
        "ghqk,gqhe->gkhe",
        chance.astype(jnp.bfloat16),
        grad_heads,
        preferred_element_type=jnp.float32,
    )
    chance_grad = jnp.einsum(
        "gqhe,gkhe->ghqk", grad_heads, split_heads(values), preferred_element_type=jnp.float32
    )
    scores_grad = (
        chance * (chance_grad - jnp.sum(chance * chance_grad, axis=-1, keepdims=True))
    ).astype(jnp.bfloat16)
    query_grad = jnp.einsum(
        "ghqk,gkhe->gqhe", scores_grad, split_heads(keys), preferred_element_type=jnp.float32
    ) * HEAD_DIM ** (-0.5)
    keys_grad = jnp.einsum(
        "ghqk,gqhe->gkhe", scores_grad, split_heads(query), preferred_element_type=jnp.float32
    ) * HEAD_DIM ** (-0.5)
    return (
        query_grad.reshape(query.shape),
        keys_grad.reshape(keys.shape),
        values_grad.reshape(values.shape),
    )


def gelu_slope(hidden):
    return (
        0.5 * (1.0 + lax.erf(hidden * 0.7071067811865476))
        + hidden * jnp.exp(-0.5 * hidden * hidden) * 0.3989422804014327
    )


def tail_forward(resid, mixed, output, expand, shrink, gains, shifts):
    first, normed_one, inverse_one = norm_forward(
        resid + forward_dot(mixed, output), gains[0], shifts[0]
    )
    first_low = first.astype(jnp.bfloat16)
    hidden = forward_dot(first_low, expand)
    active = jax.nn.gelu(hidden, approximate=False).astype(jnp.bfloat16)
    second, normed_two, inverse_two = norm_forward(
        first + forward_dot(active, shrink), gains[1], shifts[1]
    )
    return (second, (normed_one, inverse_one, first_low, hidden, active, normed_two, inverse_two))


def tail_backward(grad, kept, output, expand, shrink, gains):
    normed_one, inverse_one, first_low, hidden, active, normed_two, inverse_two = kept
    second_grad, gain_two, shift_two = norm_backward(grad, normed_two, inverse_two, gains[1])
    branch_low = second_grad.astype(jnp.bfloat16)
    hidden_grad = (against_dot(branch_low, shrink) * gelu_slope(hidden)).astype(jnp.bfloat16)
    first_grad, gain_one, shift_one = norm_backward(
        second_grad + against_dot(hidden_grad, expand), normed_one, inverse_one, gains[0]
    )
    attend_low = first_grad.astype(jnp.bfloat16)
    mixed_grad = against_dot(attend_low, output).astype(jnp.bfloat16)
    return (
        first_grad,
        mixed_grad,
        (branch_low, hidden_grad, attend_low),
        jnp.stack([gain_one, gain_two]),
        jnp.stack([shift_one, shift_two]),
    )


def tail_mats(mixed, kept, factors):
    branch_low, hidden_grad, attend_low = factors
    return (
        across_dot(mixed, attend_low),
        across_dot(kept[2], hidden_grad),
        across_dot(kept[4], branch_low),
    )


def per_device(
    tokens,
    cotangent,
    document_ids,
    inner_project,
    inner_output,
    inner_expand,
    inner_shrink,
    inner_gains,
    inner_shifts,
    outer_project,
    outer_output,
    outer_expand,
    outer_shrink,
    outer_gains,
    outer_shifts,
    position_table,
):
    rows = tokens.shape[1]
    width = tokens.shape[2]
    local_segs = rows // SEG_LEN
    parts = lax.axis_size("seg")
    here = lax.axis_index("seg")
    inner = (
        lax.all_gather(inner_project, "seg", axis=0, tiled=True),
        lax.all_gather(inner_output, "seg", axis=0, tiled=True),
        lax.all_gather(inner_expand, "seg", axis=0, tiled=True),
        lax.all_gather(inner_shrink, "seg", axis=0, tiled=True),
    )
    source = tokens[0]
    triple = (
        forward_dot(source, inner[0]).astype(jnp.bfloat16).reshape(local_segs, SEG_LEN, 3 * width)
    )
    query = triple[..., :width]
    keys = triple[..., width : 2 * width]
    values = triple[..., 2 * width :]
    mixed, log_total = attend_forward(query, keys, values, None)
    mixed = mixed.reshape(rows, width)
    settled, kept = tail_forward(
        source.astype(jnp.float32), mixed, inner[1], inner[2], inner[3], inner_gains, inner_shifts
    )
    framed = settled.reshape(local_segs, SEG_LEN, width)
    summary_own = framed[:, 0, :].astype(jnp.bfloat16)
    cot_frames = cotangent[0].reshape(local_segs, SEG_LEN, width)
    summary_cot = cot_frames[:, 0, :]
    doc_row = document_ids[0]
    count = doc_row.shape[0]
    before = jnp.sum((doc_row[None, :] < doc_row[:, None]).astype(jnp.int32), axis=1)
    places = jnp.arange(count, dtype=jnp.int32) - before
    onehot = (
        places[:, None] == jnp.arange(position_table.shape[0], dtype=jnp.int32)[None, :]
    ).astype(jnp.float32)
    outer = (
        lax.all_gather(outer_project, "seg", axis=0, tiled=True),
        lax.all_gather(outer_output, "seg", axis=0, tiled=True),
        lax.all_gather(outer_expand, "seg", axis=0, tiled=True),
        lax.all_gather(outer_shrink, "seg", axis=0, tiled=True),
    )
    start = here * local_segs
    mat_rows = width // parts
    table_rows = position_table.shape[0] // parts
    summary_all, cot_all = (
        lax.all_gather(summary_own, "seg", axis=0, tiled=True),
        lax.all_gather(summary_cot, "seg", axis=0, tiled=True),
    )
    allowed = (doc_row[:, None] == doc_row[None, :])[None]
    resid = summary_all.astype(jnp.float32) + forward_dot(
        onehot.astype(jnp.bfloat16), position_table
    )
    resid_low = resid.astype(jnp.bfloat16)
    outer_triple = forward_dot(resid_low, outer[0]).astype(jnp.bfloat16)
    outer_query = outer_triple[None, :, :width]
    outer_keys = outer_triple[None, :, width : 2 * width]
    outer_values = outer_triple[None, :, 2 * width :]
    outer_mixed, outer_total = attend_forward(outer_query, outer_keys, outer_values, allowed)
    merged_all, outer_kept = tail_forward(
        resid, outer_mixed[0], outer[1], outer[2], outer[3], outer_gains, outer_shifts
    )
    back_resid, back_mixed, outer_factors, outer_gain_grad, outer_shift_grad = tail_backward(
        cot_all.astype(jnp.float32), outer_kept, outer[1], outer[2], outer[3], outer_gains
    )
    outer_mats = tail_mats(outer_mixed[0], outer_kept, outer_factors)
    query_grad, keys_grad, values_grad = attend_backward(
        back_mixed[None], outer_query, outer_keys, outer_values, allowed, outer_total
    )
    outer_triple_grad = jnp.concatenate(
        [query_grad[0], keys_grad[0], values_grad[0]], axis=1
    ).astype(jnp.bfloat16)
    summary_all_grad = back_resid + against_dot(outer_triple_grad, outer[0])
    merged = lax.dynamic_slice_in_dim(merged_all, start, local_segs)
    summary_grad = lax.dynamic_slice_in_dim(summary_all_grad, start, local_segs)
    wide_rows = outer_mats[2].shape[0] // parts
    outer_grads = (
        lax.dynamic_slice_in_dim(
            across_dot(resid_low, outer_triple_grad), here * mat_rows, mat_rows
        ),
        lax.dynamic_slice_in_dim(outer_mats[0], here * mat_rows, mat_rows),
        lax.dynamic_slice_in_dim(outer_mats[1], here * mat_rows, mat_rows),
        lax.dynamic_slice_in_dim(outer_mats[2], here * wide_rows, wide_rows),
        lax.dynamic_slice_in_dim(outer_gain_grad, here * mat_rows, mat_rows, axis=1),
        lax.dynamic_slice_in_dim(outer_shift_grad, here * mat_rows, mat_rows, axis=1),
        lax.dynamic_slice_in_dim(
            table_sum(onehot, summary_all_grad), here * table_rows, table_rows
        ),
    )
    layer_output = framed.at[:, 0, :].set(merged).reshape(rows, width).astype(jnp.bfloat16)
    tail_grad = cot_frames.astype(jnp.float32).at[:, 0, :].set(summary_grad).reshape(rows, width)
    first_grad, mixed_grad, inner_factors, inner_gain_grad, inner_shift_grad = tail_backward(
        tail_grad, kept, inner[1], inner[2], inner[3], inner_gains
    )
    inner_mats = tail_mats(mixed, kept, inner_factors)
    query_grad, keys_grad, values_grad = attend_backward(
        mixed_grad.reshape(local_segs, SEG_LEN, width), query, keys, values, None, log_total
    )
    triple_grad = (
        jnp.concatenate([query_grad, keys_grad, values_grad], axis=2)
        .reshape(rows, 3 * width)
        .astype(jnp.bfloat16)
    )
    tokens_grad = first_grad + against_dot(triple_grad, inner[0])
    inner_grads = (
        lax.psum_scatter(across_dot(source, triple_grad), "seg", scatter_dimension=0, tiled=True),
        lax.psum_scatter(inner_mats[0], "seg", scatter_dimension=0, tiled=True),
        lax.psum_scatter(inner_mats[1], "seg", scatter_dimension=0, tiled=True),
        lax.psum_scatter(inner_mats[2], "seg", scatter_dimension=0, tiled=True),
        lax.psum_scatter(inner_gain_grad, "seg", scatter_dimension=1, tiled=True),
        lax.psum_scatter(inner_shift_grad, "seg", scatter_dimension=1, tiled=True),
    )
    totals = (
        lax.psum(inner_grads[0].astype(jnp.bfloat16), "docs").astype(jnp.float32),
        lax.psum(inner_grads[1].astype(jnp.bfloat16), "docs").astype(jnp.float32),
        lax.psum(inner_grads[2].astype(jnp.bfloat16), "docs").astype(jnp.float32),
        lax.psum(inner_grads[3].astype(jnp.bfloat16), "docs").astype(jnp.float32),
        lax.psum(inner_grads[4].astype(jnp.bfloat16), "docs").astype(jnp.float32),
        lax.psum(inner_grads[5].astype(jnp.bfloat16), "docs").astype(jnp.float32),
        lax.psum(outer_grads[0].astype(jnp.bfloat16), "docs").astype(jnp.float32),
        lax.psum(outer_grads[1].astype(jnp.bfloat16), "docs").astype(jnp.float32),
        lax.psum(outer_grads[2].astype(jnp.bfloat16), "docs").astype(jnp.float32),
        lax.psum(outer_grads[3].astype(jnp.bfloat16), "docs").astype(jnp.float32),
        lax.psum(outer_grads[4].astype(jnp.bfloat16), "docs").astype(jnp.float32),
        lax.psum(outer_grads[5].astype(jnp.bfloat16), "docs").astype(jnp.float32),
        lax.psum(outer_grads[6].astype(jnp.bfloat16), "docs").astype(jnp.float32),
    )
    return (
        layer_output[None],
        tokens_grad[None],
        totals[0],
        totals[1],
        totals[2],
        totals[3],
        totals[4],
        totals[5],
        totals[6],
        totals[7],
        totals[8],
        totals[9],
        totals[10],
        totals[11],
        totals[12],
    )


SEG = 128
ROWS = 512
D = 768
FF = 3072
SLICE = 96
AXES = ("docs", "seg")
bf16 = jnp.bfloat16
f32 = jnp.float32
NEXT = (1, 3, 0, 2)


def dot(a, b):
    return jnp.dot(a, b, preferred_element_type=f32)


def dot_bt(a, b):
    return lax.dot_general(a, b, (((1,), (1,)), ((), ())), preferred_element_type=f32)


def dot_at(a, b):
    return lax.dot_general(a, b, (((0,), (0,)), ((), ())), preferred_element_type=f32)


def place_of(docs, seg):
    after = jnp.where(docs == 0, 1, jnp.where(docs == 1, 3, jnp.where(docs == 3, 2, 0)))
    return (seg // 2, seg % 2, docs, after)


def slot_of(target, docs, after):
    return jnp.where(
        target == docs, 0, jnp.where(target == 3 - after, 1, jnp.where(target == after, 2, 3))
    )


def here():
    return place_of(lax.axis_index("docs"), lax.axis_index("seg"))


def cols(start, size):
    return pl.ds(pl.multiple_of(start, 128), size)


def start_block(kind, target, refs, dst, sem, column=0):
    z, c, docs, after = here()
    slot = slot_of(target, docs, after)
    for core in range(2):
        own, ext = refs[core], refs[2 + core]
        cc = c if core == 0 else 1 - c
        for k in range(4):
            seg = 2 * lax.rem(z + 4 - k, 4) + cc
            if kind == "rows":
                at = pl.ds(pl.multiple_of(seg * 4 * SLICE + target * SLICE, SLICE), SLICE)
            else:
                at = pl.ds(pl.multiple_of(seg * SLICE, SLICE), SLICE)
            if k == 0:
                if kind == "rows":
                    src = own.at[pl.ds(target * SLICE, SLICE), :]
                else:
                    src = own.at[:, pl.ds(target * D, D)]
            else:
                row = pl.multiple_of(slot * (3 * SLICE) + (k - 1) * SLICE, SLICE)
                src = ext.at[pl.ds(row, SLICE), pl.ds(column, D)]
            pltpu.make_async_copy(src, dst.at[at, :], sem).start()


def wait_all(buf, sem):
    pltpu.make_async_copy(buf, buf, sem).wait()


def norm_rows(x, gain, shift):
    center = x - jnp.mean(x, axis=-1, keepdims=True)
    inverse = lax.rsqrt(jnp.mean(center * center, axis=-1, keepdims=True) + EPS)
    normed = center * inverse
    return normed * gain + shift, normed, inverse


def norm_rows_back(grad, normed, inverse, gain):
    scaled = grad * gain
    return inverse * (
        scaled
        - jnp.mean(scaled, axis=-1, keepdims=True)
        - normed * jnp.mean(scaled * normed, axis=-1, keepdims=True)
    )


def gelu_both(h):
    upper = 0.5 * (1.0 + lax.erf(h * 0.7071067811865476))
    return h * upper, upper + h * jnp.exp(-0.5 * h * h) * 0.3989422804014327


def low_lanes(shape):
    return lax.broadcasted_iota(jnp.int32, shape, 1) < HEAD_DIM


def stack_heads(pair):
    left = low_lanes(pair.shape)
    zero = jnp.zeros_like(pair)
    return jnp.concatenate([jnp.where(left, pair, zero), jnp.where(left, zero, pair)], axis=0)


def unstack_heads(both):
    half = both.shape[0] // 2
    top, bottom = both[:half], both[half:]
    return jnp.where(low_lanes(top.shape), top, bottom)


def attend_unit(query, keys, values, allowed):
    scores = dot_bt(stack_heads(query), keys) * HEAD_DIM ** (-0.5)
    if allowed is not None:
        scores = jnp.where(allowed, scores, LOWEST)
    raised = jnp.exp(scores - jnp.max(scores, axis=-1, keepdims=True))
    chance = (raised / jnp.sum(raised, axis=-1, keepdims=True)).astype(bf16)
    return chance, unstack_heads(dot(chance, values)).astype(bf16)


def attend_unit_back(chance, grad, query, keys, values):
    spread = stack_heads(grad)
    wide = chance.astype(f32)
    chance_grad = dot_bt(spread, values)
    scores_grad = (
        wide * (chance_grad - jnp.sum(wide * chance_grad, axis=-1, keepdims=True))
    ).astype(bf16)
    scale = HEAD_DIM ** (-0.5)
    return (
        (unstack_heads(dot(scores_grad, keys)) * scale).astype(bf16),
        (dot_at(scores_grad, stack_heads(query)) * scale).astype(bf16),
        dot_at(chance, spread).astype(bf16),
    )


def kernel_attend(src, po, mpo, ext, mext, gains, shifts, triple, chance, mixed, first, norm, inv, low, w, sem):
    for t in range(4):
        start_block("cols", t, (po, mpo, ext, mext), w.at[t], sem.at[t])
    for t in range(3):
        wait_all(w.at[t], sem.at[t])

        @pl.loop(0, 3)
        def _(j):
            triple[:, cols(t * D + j * 256, 256)] = dot(src[...], w[t, :, cols(j * 256, 256)]).astype(bf16)

    @pl.loop(0, 24)
    def _(u):
        at = pl.ds(pl.multiple_of(u // 6 * SEG, SEG), SEG)
        p = u % 6 * 128
        probs, out = attend_unit(
            triple[at, cols(p, 128)], triple[at, cols(p + D, 128)], triple[at, cols(p + 2 * D, 128)], None
        )
        chance[u] = probs
        mixed[at, cols(p, 128)] = out

    wait_all(w.at[3], sem.at[3])

    @pl.loop(0, 3)
    def _(j):
        at = cols(j * 256, 256)
        first[:, at] = src[:, at].astype(f32) + dot(mixed[...], w[3, :, at])

    @pl.loop(0, ROWS // 64)
    def _(r):
        at = pl.ds(pl.multiple_of(r * 64, 64), 64)
        out, normed, inverse = norm_rows(first[at, :], gains[0:1, :], shifts[0:1, :])
        first[at, :] = out
        norm[at, :] = normed
        inv[at, :] = jnp.broadcast_to(inverse, (64, 128))
        low[at, :] = out.astype(bf16)


def kernel_expand(low, e, me, ext, mext, active, slope, w, sem):
    for t in range(4):
        start_block("cols", t, (e, me, ext, mext), w.at[t], sem.at[t])
    for t in range(4):
        wait_all(w.at[t], sem.at[t])

        @pl.loop(0, 3)
        def _(j):
            h = dot(low[...], w[t, :, cols(j * 256, 256)])
            a, b = gelu_both(h)
            at = cols(t * D + j * 256, 256)
            active[:, at] = a.astype(bf16)
            slope[:, at] = b.astype(bf16)


def kernel_shrink(active, first, mixed, src, cot, marks, s, ms, ext, mext, gains, shifts, out, norm, inv, payload, w, x, sem):
    for t in range(4):
        start_block("rows", t, (s, ms, ext, mext), w, sem.at[0])
    wait_all(w, sem.at[0])

    @pl.loop(0, 3)
    def _(j):
        at = cols(j * 256, 256)
        x[:, at] = first[:, at] + dot(active[...], w[:, at])

    @pl.loop(0, ROWS // 64)
    def _(r):
        at = pl.ds(pl.multiple_of(r * 64, 64), 64)
        res, normed, inverse = norm_rows(x[at, :], gains[1:2, :], shifts[1:2, :])
        norm[at, :] = normed
        inv[at, :] = jnp.broadcast_to(inverse, (64, 128))
        out[at, :] = res.astype(bf16)

    for n, ref in enumerate((out, cot, src, mixed)):
        lines = [ref[s4 * SEG : s4 * SEG + 16, :].astype(f32)[0:1] for s4 in range(4)]
        payload[:, n * D : (n + 1) * D] = jnp.concatenate(lines, axis=0).astype(bf16)
    payload[:, 4 * D : 4 * D + 128] = marks[...]


def kernel_back(cot, norm2, inv2, norm1, inv1, slope, s, ms, sext, msext, e, me, eext, meext, po, mpo, aext, maext, gains,
                branch_low, hidden_grad, first_grad, attend_low, mixed_grad, sums, ws, we, wo, second, acc, sem):
    for t in range(4):
        start_block("rows", t, (s, ms, sext, msext), ws, sem.at[0])
    for t in range(4):
        start_block("cols", t, (e, me, eext, meext), we.at[t], sem.at[1 + t])
    start_block("cols", 3, (po, mpo, aext, maext), wo, sem.at[5])
    acc[...] = jnp.zeros_like(acc)

    def back_one(r, carry):
        gain_sum, shift_sum = carry
        at = pl.ds(pl.multiple_of(r * 64, 64), 64)
        line = lax.broadcasted_iota(jnp.int32, (64, 1), 0) + r * 64
        grad = jnp.where(line % SEG == 0, 0.0, cot[at, :].astype(f32))
        normed = norm2[at, :]
        res = norm_rows_back(grad, normed, inv2[at, 0:1], gains[1:2, :])
        second[at, :] = res
        branch_low[at, :] = res.astype(bf16)
        return (
            gain_sum + jnp.sum(grad * normed, axis=0, keepdims=True),
            shift_sum + jnp.sum(grad, axis=0, keepdims=True),
        )

    zero = jnp.zeros((1, D), f32)
    gain_two, shift_two = lax.fori_loop(0, ROWS // 64, back_one, (zero, zero))
    wait_all(ws, sem.at[0])
    for t in range(4):
        wait_all(we.at[t], sem.at[1 + t])

        @pl.loop(0, 3)
        def _(j):
            at = cols(t * D + j * 256, 256)
            rows = pl.ds(pl.multiple_of(t * D + j * 256, 256), 256)
            grad = (dot_bt(branch_low[...], ws[rows, :]) * slope[:, at].astype(f32)).astype(bf16)
            hidden_grad[:, at] = grad

        @pl.loop(0, 3)
        def _(j):
            rows = pl.ds(pl.multiple_of(j * 256, 256), 256)
            at = cols(j * 256, 256)
            acc[:, at] += dot_bt(hidden_grad[:, t * D : (t + 1) * D], we[t, rows, :])

    def back_two(r, carry):
        gain_sum, shift_sum = carry
        at = pl.ds(pl.multiple_of(r * 64, 64), 64)
        grad = second[at, :] + acc[at, :]
        normed = norm1[at, :]
        res = norm_rows_back(grad, normed, inv1[at, 0:1], gains[0:1, :])
        first_grad[at, :] = res
        attend_low[at, :] = res.astype(bf16)
        return (
            gain_sum + jnp.sum(grad * normed, axis=0, keepdims=True),
            shift_sum + jnp.sum(grad, axis=0, keepdims=True),
        )

    gain_one, shift_one = lax.fori_loop(0, ROWS // 64, back_two, (zero, zero))
    sums[...] = jnp.concatenate(
        [gain_one, gain_two, shift_one, shift_two, jnp.zeros((4, D), f32)], axis=0
    )
    wait_all(wo, sem.at[5])

    @pl.loop(0, 3)
    def _(j):
        rows = pl.ds(pl.multiple_of(j * 256, 256), 256)
        mixed_grad[:, cols(j * 256, 256)] = dot_bt(attend_low[...], wo[rows, :]).astype(bf16)


def kernel_shrink_grad(active, branch_low, sums, keep, send):
    core = lax.axis_index("seg") % 2
    extra = sums[...].astype(bf16)

    @pl.loop(0, 4)
    def _(z):
        for which, out in ((core, keep), (1 - core, send)):
            seg = 2 * z + which
            value = dot_at(active[:, cols(seg * (4 * SLICE), 4 * SLICE)], branch_low[...]).astype(bf16)
            for t in range(4):
                out[t, z, :SLICE, :] = value[t * SLICE : (t + 1) * SLICE, :]
                out[t, z, SLICE:, :] = extra


def kernel_expand_grad(low, hidden_grad, keep, send, turned):
    core = lax.axis_index("seg") % 2
    for i in range(6):
        turned[i * 128 : (i + 1) * 128, :] = low[:, i * 128 : (i + 1) * 128].T

    @pl.loop(0, 12)
    def _(n):
        value = dot(turned[...], hidden_grad[:, cols(n * 256, 256)]).astype(bf16)
        for i in range(8):
            piece = value[i * SLICE : (i + 1) * SLICE, :]

            @pl.when(core == i % 2)
            def _():
                keep[n // 3, i // 2, :, cols(n % 3 * 256, 256)] = piece

            @pl.when(core != i % 2)
            def _():
                send[n // 3, i // 2, :, cols(n % 3 * 256, 256)] = piece


def kernel_attend_back(triple, chance, mixed_grad, fix, src, mixed, attend_low, triple_grad, keep, send, turned):
    core = lax.axis_index("seg") % 2
    first_line = lax.broadcasted_iota(jnp.int32, (SEG, 128), 0) == 0

    @pl.loop(0, 24)
    def _(u):
        s4 = u // 6
        at = pl.ds(pl.multiple_of(s4 * SEG, SEG), SEG)
        p = u % 6 * 128
        grad = mixed_grad[at, cols(p, 128)].astype(f32)
        grad = jnp.where(first_line, fix[s4, 0:1, cols(p, 128)], grad).astype(bf16)
        gq, gk, gv = attend_unit_back(
            chance[u], grad, triple[at, cols(p, 128)], triple[at, cols(p + D, 128)], triple[at, cols(p + 2 * D, 128)]
        )
        triple_grad[at, cols(p, 128)] = gq
        triple_grad[at, cols(p + D, 128)] = gk
        triple_grad[at, cols(p + 2 * D, 128)] = gv

    def store(t, j, value):
        low = value.astype(bf16)
        for i in range(8):
            piece = low[i * SLICE : (i + 1) * SLICE, :]

            @pl.when(core == i % 2)
            def _():
                keep[t, i // 2, :, cols(j * 256, 256)] = piece

            @pl.when(core != i % 2)
            def _():
                send[t, i // 2, :, cols(j * 256, 256)] = piece

    for i in range(6):
        turned[i * 128 : (i + 1) * 128, :] = src[:, i * 128 : (i + 1) * 128].T

    @pl.loop(0, 9)
    def _(n):
        store(n // 3, n % 3, dot(turned[...], triple_grad[:, cols(n * 256, 256)]))

    for i in range(6):
        turned[i * 128 : (i + 1) * 128, :] = mixed[:, i * 128 : (i + 1) * 128].T

    @pl.loop(0, 3)
    def _(n):
        store(3, n, dot(turned[...], attend_low[:, cols(n * 256, 256)]))


def kernel_tokens_grad(triple_grad, first_grad, fix, po, mpo, ext, mext, out, w, sem):
    for t in range(3):
        start_block("cols", t, (po, mpo, ext, mext), w.at[t], sem.at[t])
    for t in range(3):
        wait_all(w.at[t], sem.at[t])

    @pl.loop(0, 3)
    def _(j):
        rows = pl.ds(pl.multiple_of(j * 256, 256), 256)
        at = cols(j * 256, 256)
        value = first_grad[:, at]
        for t in range(3):
            value += dot_bt(triple_grad[:, t * D : (t + 1) * D], w[t, rows, :])
        out[:, at] = value

    for s4 in range(4):
        out[s4 * SEG : s4 * SEG + 1, :] += fix[s4 : s4 + 1, :]


def tail_both(x, mixed, grad_of, wo, we, ws, gains, shifts, first, norm, low, slope, acc,
              active, branch_low, hidden_grad, attend_low, sums, merged):
    @pl.loop(0, 3)
    def _(j):
        at = cols(j * 256, 256)
        x[:, at] += dot(mixed[...], wo[:, at])

    out, normed, inverse_one = norm_rows(x[...], gains[0:1, :], shifts[0:1, :])
    first[...] = out
    norm[...] = normed
    low[...] = out.astype(bf16)

    @pl.loop(0, 12)
    def _(j):
        a, b = gelu_both(dot(low[...], we[j // 3, :, cols(j % 3 * 256, 256)]))
        at = cols(j * 256, 256)
        active[:, at] = a.astype(bf16)
        slope[:, at] = b

    @pl.loop(0, 3)
    def _(j):
        at = cols(j * 256, 256)
        x[:, at] = first[:, at] + dot(active[...], ws[:, at])

    out, normed, inverse_two = norm_rows(x[...], gains[1:2, :], shifts[1:2, :])
    if merged is not None:
        merged[...] = out[:8]
    grad = grad_of()
    gain_two = jnp.sum(grad * normed, axis=0, keepdims=True)
    shift_two = jnp.sum(grad, axis=0, keepdims=True)
    second = norm_rows_back(grad, normed, inverse_two, gains[1:2, :])
    acc[...] = second
    branch_low[...] = second.astype(bf16)

    @pl.loop(0, 12)
    def _(j):
        at = cols(j * 256, 256)
        rows = pl.ds(pl.multiple_of(j * 256, 256), 256)
        hidden_grad[:, at] = (dot_bt(branch_low[...], ws[rows, :]) * slope[:, at]).astype(bf16)

    for t in range(4):

        @pl.loop(0, 3)
        def _(j):
            rows = pl.ds(pl.multiple_of(j * 256, 256), 256)
            acc[:, cols(j * 256, 256)] += dot_bt(hidden_grad[:, t * D : (t + 1) * D], we[t, rows, :])

    grad = acc[...]
    normed = norm[...]
    gain_one = jnp.sum(grad * normed, axis=0, keepdims=True)
    shift_one = jnp.sum(grad, axis=0, keepdims=True)
    res = norm_rows_back(grad, normed, inverse_one, gains[0:1, :])
    acc[...] = res
    attend_low[...] = res.astype(bf16)
    sums[...] = jnp.concatenate(
        [gain_one, gain_two, shift_one, shift_two, jnp.zeros((4, D), f32)], axis=0
    )


def kernel_outer(rows, table, po, mpo, e, me, s, ms, ext, mext, gains, shifts,
                 merged, out, resid_low, triple_grad, mixed, attend_low, low, hidden_grad, active, branch_low, sums,
                 wa, we, ws, x, triple, chance, first, norm, slope, acc, mixed_grad, sem):
    for t in range(4):
        start_block("cols", t, (po, mpo, ext, mext), wa.at[t], sem.at[t], 0)
    for t in range(4):
        start_block("cols", t, (e, me, ext, mext), we.at[t], sem.at[4 + t], D)
    for t in range(4):
        start_block("rows", t, (s, ms, ext, mext), ws, sem.at[8], 2 * D)
    marks = rows[:, 4 * D : 4 * D + 128].astype(f32)
    key = jnp.broadcast_to(marks[:, 0:1], (128, 128))
    allowed = key == key.T
    allowed = jnp.concatenate([allowed, allowed], axis=0)
    onehot = (marks[:, 1:2].astype(jnp.int32) == lax.broadcasted_iota(jnp.int32, (128, 64), 1)).astype(bf16)
    resid = rows[:, :D].astype(f32) + dot(onehot, table[...])
    x[...] = resid
    resid_low[...] = resid.astype(bf16)
    for t in range(3):
        wait_all(wa.at[t], sem.at[t])

        @pl.loop(0, 3)
        def _(j):
            triple[:, cols(t * D + j * 256, 256)] = dot(resid_low[...], wa[t, :, cols(j * 256, 256)]).astype(bf16)

    @pl.loop(0, 6)
    def _(u):
        p = u * 128
        probs, value = attend_unit(triple[:, cols(p, 128)], triple[:, cols(p + D, 128)], triple[:, cols(p + 2 * D, 128)], allowed)
        chance[u] = probs
        mixed[:, cols(p, 128)] = value

    wait_all(wa.at[3], sem.at[3])
    for t in range(4):
        wait_all(we.at[t], sem.at[4 + t])
    wait_all(ws, sem.at[8])
    tail_both(x, mixed, lambda: rows[:, D : 2 * D].astype(f32), wa.at[3], we, ws, gains, shifts, first, norm, low,
              slope, acc, active, branch_low, hidden_grad, attend_low, sums, merged)

    @pl.loop(0, 3)
    def _(j):
        at = pl.ds(pl.multiple_of(j * 256, 256), 256)
        mixed_grad[:, cols(j * 256, 256)] = dot_bt(attend_low[...], wa[3, at, :]).astype(bf16)

    @pl.loop(0, 6)
    def _(u):
        p = u * 128
        gq, gk, gv = attend_unit_back(chance[u], mixed_grad[:, cols(p, 128)], triple[:, cols(p, 128)],
                                      triple[:, cols(p + D, 128)], triple[:, cols(p + 2 * D, 128)])
        triple_grad[:, cols(p, 128)] = gq
        triple_grad[:, cols(p + D, 128)] = gk
        triple_grad[:, cols(p + 2 * D, 128)] = gv

    @pl.loop(0, 3)
    def _(j):
        at = pl.ds(pl.multiple_of(j * 256, 256), 256)
        value = acc[:, cols(j * 256, 256)]
        for t in range(3):
            value += dot_bt(triple_grad[:, t * D : (t + 1) * D], wa[t, at, :])
        out[:, cols(j * 256, 256)] = value


def kernel_heads(rows, grad, po, mpo, aext, maext, e, me, eext, meext, s, ms, sext, msext, gains, shifts,
                 first_fix, mixed_fix, attend_low, low, hidden_grad, active, branch_low, sums,
                 wo, we, ws, x, mixed, first, norm, slope, acc, sem):
    start_block("cols", 3, (po, mpo, aext, maext), wo, sem.at[0])
    for t in range(4):
        start_block("cols", t, (e, me, eext, meext), we.at[t], sem.at[1 + t])
    for t in range(4):
        start_block("rows", t, (s, ms, sext, msext), ws, sem.at[5])
    x[...] = rows[:, 2 * D : 3 * D].astype(f32)
    mixed[...] = rows[:, 3 * D : 4 * D]
    wait_all(wo, sem.at[0])
    for t in range(4):
        wait_all(we.at[t], sem.at[1 + t])
    wait_all(ws, sem.at[5])
    tail_both(x, mixed, lambda: grad[...], wo, we, ws, gains, shifts, first, norm, low,
              slope, acc, active, branch_low, hidden_grad, attend_low, sums, None)
    first_fix[...] = acc[:8, :]

    @pl.loop(0, 3)
    def _(j):
        at = pl.ds(pl.multiple_of(j * 256, 256), 256)
        value = dot_bt(attend_low[0:16, :], wo[at, :])
        for s4 in range(4):
            mixed_fix[s4, :, cols(j * 256, 256)] = jnp.broadcast_to(value[s4 : s4 + 1], (8, 256))


def kernel_small_grads(rows, grad, resid_low, triple_grad, mixed_o, attend_o, low_o, hidden_o, active_o, branch_o,
                       attend_f, low_f, hidden_f, active_f, branch_f,
                       project, output, expand, shrink, output_f, expand_f, shrink_f, table_grad, turned, whole):
    seg = lax.axis_index("seg")
    own = pl.ds(pl.multiple_of(seg * SLICE, 32), SLICE)
    wide = cols(seg * (4 * SLICE), 4 * SLICE)

    for n, ref in enumerate((resid_low, mixed_o, low_o, low_f)):
        turned[n] = ref[...].T
    turned[4] = rows[:, 3 * D : 4 * D].T
    left, left_mixed, left_o, left_f, left_head = (turned[n, own, :] for n in range(5))

    @pl.loop(0, 9)
    def _(j):
        project[:, cols(j * 256, 256)] = dot(left, triple_grad[:, cols(j * 256, 256)])

    output[...] = dot(left_mixed, attend_o[...])
    output_f[...] = dot(left_head, attend_f[...])

    @pl.loop(0, 12)
    def _(j):
        expand[:, cols(j * 256, 256)] = dot(left_o, hidden_o[:, cols(j * 256, 256)])

    @pl.loop(0, 12)
    def _(j):
        expand_f[:, cols(j * 256, 256)] = dot(left_f, hidden_f[:, cols(j * 256, 256)])

    @pl.loop(0, 3)
    def _(j):
        at = cols(j * 256, 256)
        shrink[:, at] = dot_at(active_o[:, wide], branch_o[:, at])
        shrink_f[:, at] = dot_at(active_f[:, wide], branch_f[:, at])

    marks = rows[:, 4 * D : 4 * D + 128].astype(f32)
    onehot = (marks[:, 1:2].astype(jnp.int32) == lax.broadcasted_iota(jnp.int32, (128, 64), 1)).astype(f32)
    whole[...] = lax.dot_general(onehot, grad[...], (((0,), (0,)), ((), ())), precision=HIGH, preferred_element_type=f32)
    table_grad[...] = whole[pl.ds(pl.multiple_of(seg * 8, 8), 8), :]


def call(kernel, where, outs, scratch, *args):
    spec = {"v": pl.BlockSpec(memory_space=pltpu.VMEM), "h": pl.BlockSpec(memory_space=pl.ANY)}
    moved = sum(a.size * a.dtype.itemsize for a in args)
    return pl.pallas_call(
        kernel,
        out_shape=tuple(jax.ShapeDtypeStruct(s, t) for s, t in outs),
        in_specs=[spec[letter] for letter in where],
        out_specs=tuple(pl.BlockSpec(memory_space=pltpu.VMEM) for _ in outs),
        scratch_shapes=[
            pltpu.SemaphoreType.DMA((s,)) if isinstance(s, int) else pltpu.VMEM(s[0], s[1]) for s in scratch
        ],
        compiler_params=pltpu.CompilerParams(vmem_limit_bytes=60 * 1024 * 1024),
        cost_estimate=pl.CostEstimate(flops=10**10, bytes_accessed=moved, transcendentals=0),
    )(*args)


def moves(groups, parts):
    def pairs(target):
        return tuple(
            (d * parts + s, t[0] * parts + t[1]) for d in range(groups) for s in range(parts) for t in (target(d, s),)
        )

    back = {NEXT[d]: d for d in range(4)}
    return {
        "swap": pairs(lambda d, s: (d, s ^ 1)),
        "up": pairs(lambda d, s: (d, (s + 2) % parts)),
        "up2": pairs(lambda d, s: (d, (s + 4) % parts)),
        "down": pairs(lambda d, s: (d, (s - 2) % parts)),
        "right": pairs(lambda d, s: (NEXT[d], s)),
        "left": pairs(lambda d, s: (back[d], s)),
        "across": pairs(lambda d, s: (3 - d, s)),
        "x": pairs(lambda d, s: (d ^ 1, s)),
        "y": pairs(lambda d, s: (d ^ 2, s)),
    }


def fast_device(
    tokens, cotangent, document_ids, inner_project, inner_output, inner_expand, inner_shrink, inner_gains, inner_shifts,
    outer_project, outer_output, outer_expand, outer_shrink, outer_gains, outer_shifts, position_table,
):
    groups, parts = lax.axis_size("docs"), lax.axis_size("seg")
    seg, docs = lax.axis_index("seg"), lax.axis_index("docs")
    route = moves(groups, parts)
    z, c, _, after = place_of(docs, seg)

    def move(a, way):
        return lax.ppermute(a, AXES, route[way])

    def pick(a, index, axis=0):
        return lax.dynamic_index_in_dim(a, index, axis, keepdims=False)

    def spread(own):
        lines, held = own, []
        for _ in range(3):
            lines = move(lines, "up")
            held.append(lines)
        held = jnp.concatenate(held, axis=0)
        half = own.shape[1] // 2
        right, left = move(held, "right"), move(held, "left")
        far = jnp.concatenate([move(right[:, :half], "right"), move(left[:, half:], "left")], axis=1)
        ext = jnp.concatenate([held, right, left, far], axis=0)
        return ext, move(ext, "swap")

    def quarter(project_output, expand, shrink):
        return (
            lax.dynamic_slice_in_dim(project_output, docs * D, D, axis=1),
            lax.dynamic_slice_in_dim(expand, docs * D, D, axis=1),
            lax.dynamic_slice_in_dim(shrink, docs * SLICE, SLICE, axis=0),
        )

    src, cot = tokens[0], cotangent[0]
    po = jnp.concatenate([inner_project, inner_output], axis=1)
    e, s = inner_expand, inner_shrink
    qa, qe, qs = quarter(po, e, s)
    aext, maext = spread(qa)
    mpo, me, ms = move(po, "swap"), move(e, "swap"), move(s, "swap")
    eext, meext = spread(qe)
    sext, msext = spread(qs)
    a_refs = (po, mpo, aext, maext)
    e_refs = (e, me, eext, meext)
    s_refs = (s, ms, sext, msext)
    opo = jnp.concatenate([outer_project, outer_output], axis=1)
    oe, os_ = outer_expand, outer_shrink
    oext, moext = spread(jnp.concatenate(quarter(opo, oe, os_), axis=1))
    mopo, moe, mos = move(opo, "swap"), move(oe, "swap"), move(os_, "swap")

    doc_row = document_ids[0]
    count = doc_row.shape[0]
    before = jnp.sum((doc_row[None, :] < doc_row[:, None]).astype(jnp.int32), axis=1)
    places = jnp.arange(count, dtype=jnp.int32) - before
    both = jnp.stack([doc_row + 16 * docs, places], axis=1)
    marks = jnp.pad(lax.dynamic_slice_in_dim(both, seg * 4, 4), ((0, 0), (0, 126))).astype(bf16)

    big, line = (ROWS, D), (ROWS, 128)
    square, wide = ((4, D, D), bf16), ((FF, D), bf16)
    triple, chance, mixed, first, norm1, inv1, low = call(
        kernel_attend, "vhhhhvv",
        [((ROWS, 3 * D), bf16), ((24, 256, 128), bf16), (big, bf16), (big, f32), (big, f32), (line, f32), (big, bf16)],
        [square, 4], src, *a_refs, inner_gains, inner_shifts,
    )
    active, slope = call(
        kernel_expand, "vhhhh", [((ROWS, FF), bf16), ((ROWS, FF), bf16)], [square, 4], low, *e_refs
    )
    layer_low, norm2, inv2, payload = call(
        kernel_shrink, "vvvvvvhhhhvv",
        [(big, bf16), (big, f32), (line, f32), ((4, 4 * D + 128), bf16)],
        [wide, (big, f32), 1], active, first, mixed, src, cot, marks, *s_refs, inner_gains, inner_shifts,
    )
    rows = jnp.concatenate([payload, move(payload, "swap")], axis=0)
    rows = jnp.concatenate([rows, move(rows, "right"), move(rows, "left"), move(rows, "across")], axis=0)
    rows = jnp.concatenate([rows, move(rows, "up"), move(rows, "up2"), move(rows, "down")], axis=0)

    branch_low, hidden_grad, first_grad, attend_low, mixed_grad, sums = call(
        kernel_back, "vvvvvv" + "h" * 12 + "v",
        [(big, bf16), ((ROWS, FF), bf16), (big, f32), (big, bf16), (big, bf16), ((8, D), f32)],
        [wide, square, ((D, D), bf16), (big, f32), (big, f32), 6],
        cot, norm2, inv2, norm1, inv1, slope, *s_refs, *e_refs, *a_refs, inner_gains,
    )
    tall, flat = ((4, 4, SLICE + 8, D), bf16), ((4, 4, SLICE, D), bf16)
    skeep, ssend = call(kernel_shrink_grad, "vvv", [tall, tall], [], active, branch_low, sums)
    ekeep, esend = call(kernel_expand_grad, "vv", [flat, flat], [((D, ROWS), bf16)], low, hidden_grad)

    few, few_low, few_wide = ((128, D), f32), ((128, D), bf16), ((128, FF), bf16)
    (merged, summary_grad, o_resid, o_triple_grad, o_mixed, o_attend, o_low, o_hidden, o_active, o_branch, o_sums) = call(
        kernel_outer, "vvhhhhhhhhvv",
        [((8, D), f32), few, few_low, ((128, 3 * D), bf16), few_low, few_low, few_low, few_wide, few_wide, few_low,
         ((8, D), f32)],
        [square, square, wide, few, ((128, 3 * D), bf16), ((6, 256, 128), bf16), few, few, ((128, FF), f32), few, few_low, 9],
        rows, position_table, opo, mopo, oe, moe, os_, mos, oext, moext, outer_gains, outer_shifts,
    )
    (first_fix, mixed_fix, f_attend, f_low, f_hidden, f_active, f_branch, f_sums) = call(
        kernel_heads, "vv" + "h" * 12 + "vv",
        [((8, D), f32), ((4, 8, D), f32), few_low, few_low, few_wide, few_wide, few_low, ((8, D), f32)],
        [((D, D), bf16), square, wide, few, few_low, few, few, ((128, FF), f32), few, 6],
        rows, summary_grad, *a_refs, *e_refs, *s_refs, inner_gains, inner_shifts,
    )
    triple_grad, akeep, asend = call(
        kernel_attend_back, "vvvvvvv", [((ROWS, 3 * D), bf16), flat, flat], [((D, ROWS), bf16)],
        triple, chance, mixed_grad, mixed_fix, src, mixed, attend_low,
    )
    (tokens_grad,) = call(
        kernel_tokens_grad, "vvvhhhh", [(big, f32)], [((3, D, D), bf16), 3],
        triple_grad, first_grad, first_fix, *a_refs,
    )
    own, own_wide = ((SLICE, D), f32), ((SLICE, FF), f32)
    (o_project_g, o_output_g, o_expand_g, o_shrink_g, f_output_g, f_expand_g, f_shrink_g, table_g) = call(
        kernel_small_grads, "v" * 15,
        [((SLICE, 3 * D), f32), own, own_wide, ((4 * SLICE, D), f32), own, own_wide, ((4 * SLICE, D), f32), ((8, D), f32)],
        [((5, D, 128), bf16), ((64, D), f32)],
        rows, summary_grad, o_resid, o_triple_grad, o_mixed, o_attend, o_low, o_hidden, o_active, o_branch,
        f_attend, f_low, f_hidden, f_active, f_branch,
    )

    def scatter(keep, send):
        total = keep + move(send, "swap")
        total = total.reshape((2, 2) + total.shape[1:])
        y, x = docs // 2, docs % 2
        left, right = total[..., : D // 2], total[..., D // 2 :]
        left = pick(left, x, 1) + move(pick(left, 1 - x, 1), "x")
        right = pick(right, y, 0) + move(pick(right, 1 - y, 0), "y")
        left = pick(left, y) + move(pick(left, 1 - y), "y")
        right = pick(right, x) + move(pick(right, 1 - x), "x")
        mine = jnp.concatenate([left, right], axis=-1)
        held = pick(mine, (z + 3) % 4)
        for t in (2, 1, 0):
            held = move(held, "up") + pick(mine, (z + t) % 4)
        return held

    def collect(own):
        half = D // 2
        right, left = move(own, "right"), move(own, "left")
        far = jnp.concatenate([move(right[:, :half], "right"), move(left[:, half:], "left")], axis=1)
        held = jnp.stack([own, right, left, far])
        return [pick(held, slot_of(t, docs, after)).astype(f32) for t in range(4)]

    sown = scatter(skeep, ssend)
    s_blocks = collect(sown[:SLICE])
    e_blocks = collect(scatter(ekeep, esend))
    a_blocks = collect(scatter(akeep, asend))

    def columns(lines):
        return lax.dynamic_slice_in_dim(lines, seg * SLICE, SLICE, axis=1)

    inner_sums = columns(sown[SLICE:].astype(f32) + f_sums)
    outer_sums = columns(o_sums)
    heads = merged[:4].astype(bf16)[:, None]
    layer_output = layer_low.reshape(4, SEG, D).at[:, :1].set(heads).reshape(1, ROWS, D)
    return (
        layer_output,
        tokens_grad[None],
        jnp.concatenate(a_blocks[:3], axis=1),
        a_blocks[3] + f_output_g,
        jnp.concatenate(e_blocks, axis=1) + f_expand_g,
        jnp.concatenate(s_blocks, axis=0) + f_shrink_g,
        inner_sums[:2],
        inner_sums[2:4],
        o_project_g,
        o_output_g,
        o_expand_g,
        o_shrink_g,
        outer_sums[:2],
        outer_sums[2:4],
        table_g,
    )


def solution(mesh):
    def step(*args):
        tokens, ids, table = args[0], args[2], args[15]
        fits = (
            lax.axis_size("docs") == 4
            and lax.axis_size("seg") == 8
            and tokens.shape == (1, ROWS, D)
            and ids.shape == (1, 32)
            and table.shape == (64, D)
        )
        return (fast_device if fits else per_device)(*args)

    placed = (
        P("docs", "seg", None),
        P("docs", "seg", None),
        P("docs", None),
        P("seg", None),
        P("seg", None),
        P("seg", None),
        P("seg", None),
        P(),
        P(),
        P("seg", None),
        P("seg", None),
        P("seg", None),
        P("seg", None),
        P(),
        P(),
        P(),
    )
    return jax.shard_map(
        step,
        mesh=mesh,
        in_specs=placed,
        out_specs=(
            P("docs", "seg", None),
            P("docs", "seg", None),
            P("seg", None),
            P("seg", None),
            P("seg", None),
            P("seg", None),
            P(None, "seg"),
            P(None, "seg"),
            P("seg", None),
            P("seg", None),
            P("seg", None),
            P("seg", None),
            P(None, "seg"),
            P(None, "seg"),
            P("seg", None),
        ),
        check_vma=False,
    )
```
